32 devices in a mesh: expert: 8 (over z, core), hidden: 4 (over y, x).
Axes of the slice: x: 2, y: 2, z: 4, core: 2. Of those that a mesh axis runs over, the one named last changes fastest.
Arguments:
- inputs: bfloat16 [1536, 2880], P('expert', 'hidden'), may hold values from -6 to 6
- out_grad: bfloat16 [1536, 2880], P('expert', 'hidden'), may hold values from -6 to 6
- expert_ids: int32 [1536, 4], P('expert'), may hold values from 0 to 7, all different within a row; in each aligned block of 192 rows (0 to 191, 192 to 383, ...) at most 144 rows name the same one
- route_weight: float32 [1536, 4], P('expert'), may hold values from 0.1 to 1
- w_gate: bfloat16 [8, 2880, 2880], P('expert', 'hidden'), may hold values from -0.109375 to 0.109375
- w_up: bfloat16 [8, 2880, 2880], P('expert', 'hidden'), may hold values from -0.109375 to 0.109375
- w_down: bfloat16 [8, 2880, 2880], P('expert', 'hidden'), may hold values from -0.109375 to 0.109375
Outputs:
- grad_input: bfloat16 [1536, 2880], P('expert', 'hidden')
- grad_route: float32 [1536, 4], P('expert')
- grad_gate: float32 [8, 2880, 2880], P('expert', 'hidden')
- grad_up: float32 [8, 2880, 2880], P('expert', 'hidden')
- grad_down: float32 [8, 2880, 2880], P('expert', 'hidden')
The draws below stay inside these ranges and needn't reach their ends.
Inputs may be any that keep to these rules, and one draw needn't show every extreme that they name: `expert_ids`: each token names 4 different experts. Among the 192 tokens of one index of the expert axis no expert is named more than 144 times, a bound that some block reaches.
All inputs are finite; a program needn't handle non-finite values.
Results may differ from the reference program's by a relative error of at most 0.018.
Values may be sent and summed in bfloat16 or wider, within the bound.
No kernel may reach another device: no remote copies, remote signals or barrier semaphores. Data moves between devices by JAX's collectives and lax.ppermute only.
A program may use at most 128 MiB of HBM per device.

```python
import math
import jax
import jax.numpy as jnp
import numpy as np
from jax import lax

D = 2880
FF = 2880
TOP = 4
TOK_DEV = 192
EXPERTS = 8
TOKENS = 1536
CAP = 144
N_EXPERT = 8


def steps_of(rng, extent, split, least, high):
    def one(axis_at, parts):
        heights = jax.random.uniform(jax.random.fold_in(jax.random.fold_in(rng, 6), axis_at), (parts,), jnp.float32, least / len(split), high / len(split))
        return jnp.repeat(jnp.exp(heights), extent[axis_at] // parts).reshape((-1,) + (1,) * (len(extent) - axis_at - 1))

    loudness = one(*split[0])
    for cut in split[1:]:
        loudness = loudness * one(*cut)
    return loudness


def deal_out(stream_key, own, number, rows, amount, top, most, skew):
    sequence = jax.random.permutation(stream_key, amount)
    crowded, common = shares(amount, rows * top, most, skew, True), shares(amount, rows * top, most, skew, False)
    places = jnp.arange(amount)

    def named(tallies, rotation):
        used = int((tallies > 0).sum())
        fixed = max(1, used // 4)
        moved = fixed + (places - fixed + rotation * (used - fixed)) % max(1, amount - fixed)
        return jnp.zeros((amount,), jnp.int32).at[sequence[jnp.where(places < fixed, places, moved)]].set(jnp.asarray(tallies, jnp.int32))

    tallies = jnp.where(number % 4 == 0, named(crowded, number // 4), named(common, number - number // 4 - 1))
    mixed = jax.random.permutation(jax.random.fold_in(own, 3), amount)
    donor, sink = mixed[0:amount // 2 * 2:2], mixed[1:amount // 2 * 2:2]
    room = jnp.minimum(tallies[donor] - 1, most - tallies[sink]) // 2
    room = jnp.where((donor == sequence[0]) | (sink == sequence[0]) | (tallies[sink] == 0), 0, jnp.maximum(room, 0))
    moved = jax.random.randint(jax.random.fold_in(own, 4), (amount // 2,), 0, 1 << 20) % (room + 1)
    tallies = tallies.at[donor].add(-moved).at[sink].add(moved)
    members = jnp.searchsorted(jnp.cumsum(tallies), jnp.arange(rows * top), side="right").astype(jnp.int32)
    grid = members.reshape(top, rows).T
    grid = grid[jax.random.permutation(jax.random.fold_in(own, 1), rows)]
    rotation = jax.random.randint(jax.random.fold_in(own, 2), (rows, 1), 0, top)
    return jnp.take_along_axis(grid, (jnp.arange(top)[None, :] + rotation) % top, axis=1)


def shares(amount, total, limit, lean, full):
    weights = [(1 << 20) // math.isqrt(standing ** lean) + 1 for standing in range(1, amount + 1)]
    largest = limit if full else min(limit, max(-(-total // amount), total * weights[0] // sum(weights)))
    least = 1 if total - largest >= amount - 1 else 0
    holding, spare = [largest] + [least] * (amount - 1), total - largest - least * (amount - 1)
    while spare > 0:
        movable = [i for i in range(1, amount) if holding[i] < largest] or [i for i in range(1, amount) if holding[i] < limit]
        whole, remaining = sum([weights[i] for i in movable]), spare
        for i in movable:
            more = min(limit - holding[i], max(1, remaining * weights[i] // whole), spare)
            holding[i] = holding[i] + more
            spare = spare - more
    return np.array(holding)


def noise(stream_key, extent, deviation, limit, cuts=(), kind=jnp.bfloat16):
    loudness = steps_of(stream_key, extent, cuts, -0.22, 0.18) if cuts else 1.0
    array = jax.random.normal(stream_key, extent, jnp.float32) * deviation * loudness
    return jnp.minimum(jnp.maximum(array, -limit), limit).astype(kind)


def setup_inputs(seed: int = 0) -> dict:
    splits = jax.random.split(jax.random.key(seed), 8)
    inputs = noise(splits[0], (TOKENS, D), 1.0, 6.0, ((0, 8), (1, 4)))
    out_grad = noise(splits[1], (TOKENS, D), 1.0, 6.0, ((0, 8), (1, 4)))
    expert_ids_keys = jax.random.split(jax.random.fold_in(splits[2], 1), TOKENS // TOK_DEV)
    expert_ids_turns = jax.random.permutation(jax.random.fold_in(splits[2], 3), TOKENS // TOK_DEV)
    expert_ids = jax.vmap(lambda own, number: deal_out(jax.random.fold_in(splits[2], 2), own, number, TOK_DEV, EXPERTS, TOP, CAP, 2))(expert_ids_keys, expert_ids_turns).reshape((TOKENS, TOP))
    route_weight = jnp.clip(0.1 + 0.9 * jax.random.uniform(splits[3], (TOKENS, TOP), jnp.float32) ** steps_of(splits[3], (TOKENS, TOP), ((0, 8),), -0.2, 0.2), 0.1, 1.0)
    w_gate = noise(splits[4], (EXPERTS, FF, D), D ** -0.5, 0.109375, ((0, 8), (1, 4)))
    w_up = noise(splits[5], (EXPERTS, FF, D), D ** -0.5, 0.109375, ((0, 8), (1, 4)))
    w_down = noise(splits[6], (EXPERTS, FF, D), FF ** -0.5, 0.109375, ((0, 8), (1, 4)))
    return {"inputs": inputs, "out_grad": out_grad, "expert_ids": expert_ids, "route_weight": route_weight, "w_gate": w_gate, "w_up": w_up, "w_down": w_down}


def reference(inputs, out_grad, expert_ids, route_weight, w_gate, w_up, w_down):
    pairs = TOK_DEV * TOP
    ids = expert_ids.reshape(N_EXPERT, pairs).astype(jnp.int32)
    onehot = (ids[:, :, None] == jnp.arange(EXPERTS, dtype=jnp.int32)[None, None, :]).astype(jnp.int32)
    position = jnp.cumsum(onehot, axis=1) - 1
    slot = jnp.sum(onehot * position, axis=2).astype(jnp.int32)
    source = jnp.arange(N_EXPERT, dtype=jnp.int32)[:, None]
    where = (ids * (N_EXPERT * CAP) + source * CAP + slot).reshape(-1).astype(jnp.int32)
    assign = jnp.arange(N_EXPERT * pairs, dtype=jnp.int32)
    table = jnp.zeros((EXPERTS * N_EXPERT * CAP,), jnp.int32).at[where].set(assign)
    filled = jnp.zeros((EXPERTS * N_EXPERT * CAP,), jnp.int32).at[where].set(1)
    table = table.reshape(EXPERTS, N_EXPERT * CAP)
    filled = filled.reshape(EXPERTS, N_EXPERT * CAP)
    flat_weight = route_weight.reshape(-1)

    def one_expert(carry, pieces):
        grad_acc, route_acc = carry
        rows_idx, used, wg, wu, wd = pieces
        token_idx = (rows_idx // TOP).astype(jnp.int32)
        mask = used.astype(jnp.float32)
        xs = inputs[token_idx] * used.astype(jnp.bfloat16)[:, None]
        dys = out_grad[token_idx] * used.astype(jnp.bfloat16)[:, None]
        weights = flat_weight[rows_idx] * mask
        gate = jnp.dot(xs, wg.T, preferred_element_type=jnp.float32)
        up = jnp.dot(xs, wu.T, preferred_element_type=jnp.float32)
        sig = jax.nn.sigmoid(gate)
        act = gate * sig
        hidden = (act * up).astype(jnp.bfloat16)
        back = jnp.dot(dys, wd.T, preferred_element_type=jnp.float32)
        route_part = jnp.sum(hidden.astype(jnp.float32) * back, axis=1)
        grad_hidden = weights[:, None] * back
        scaled = (weights[:, None] * dys.astype(jnp.float32)).astype(jnp.bfloat16)
        gdown = jnp.dot(hidden.T, scaled, preferred_element_type=jnp.float32)
        d_gate = (grad_hidden * up * sig * (1.0 + gate * (1.0 - sig))).astype(jnp.bfloat16)
        d_up = (grad_hidden * act).astype(jnp.bfloat16)
        ggate = jnp.dot(d_gate.T, xs, preferred_element_type=jnp.float32)
        gup = jnp.dot(d_up.T, xs, preferred_element_type=jnp.float32)
        row_grad = jnp.dot(d_gate, wg, preferred_element_type=jnp.float32) + jnp.dot(d_up, wu, preferred_element_type=jnp.float32)
        grad_acc = grad_acc.at[token_idx].add(row_grad * mask[:, None])
        route_acc = route_acc.at[rows_idx].add(route_part * mask)
        return (grad_acc, route_acc), (ggate, gup, gdown)

    start = (jnp.zeros((TOKENS, D), jnp.float32), jnp.zeros((TOKENS * TOP,), jnp.float32))
    (grad_acc, route_acc), (grad_gate, grad_up, grad_down) = lax.scan(one_expert, start, (table, filled, w_gate, w_up, w_down))
    return grad_acc.astype(jnp.bfloat16), route_acc.reshape(TOKENS, TOP), grad_gate, grad_up, grad_down
```

```python
import jax
import jax.numpy as jnp
from jax import lax
from jax.sharding import PartitionSpec as P

F32 = jnp.float32
BF16 = jnp.bfloat16


def dot(a, b, ca, cb, kind=F32):
    return lax.dot_general(a, b, (((ca,), (cb,)), ((), ())), preferred_element_type=kind)


def gather_features(own):
    size = lax.axis_size("hidden")
    if size != 4:
        return lax.all_gather(own, "hidden", axis=0, tiled=True)
    share = own.shape[0]
    cut = share // 2 // 16 * 16
    flip = [[(i, i ^ m) for i in range(size)] for m in (1, 2)]
    me = lax.axis_index("hidden")
    first = lax.ppermute(own, "hidden", flip[0])
    second = lax.ppermute(own, "hidden", flip[1])
    top = lax.ppermute(second[:cut], "hidden", flip[0])
    low = lax.ppermute(first[cut:], "hidden", flip[1])
    out = jnp.zeros((size * share, own.shape[1]), own.dtype)
    out = lax.dynamic_update_slice(out, own, (me * share, 0))
    out = lax.dynamic_update_slice(out, first, ((me ^ 1) * share, 0))
    out = lax.dynamic_update_slice(out, second, ((me ^ 2) * share, 0))
    out = lax.dynamic_update_slice(out, top, ((me ^ 3) * share, 0))
    return lax.dynamic_update_slice(out, low, ((me ^ 3) * share + cut, 0))


def per_device(inputs, out_grad, expert_ids, route_weight, w_gate, w_up, w_down):
    groups = lax.axis_size("expert")
    local_count = w_gate.shape[0]
    experts = local_count * groups
    tok, top = expert_ids.shape
    cap = 3 * top * tok // (2 * experts)
    rows = groups * cap
    tokens = groups * tok
    routing = jnp.concatenate([expert_ids.astype(F32), route_weight], axis=1)
    routing = lax.all_gather(routing, "expert", axis=0, tiled=True)
    all_x = lax.all_gather(inputs, "expert", axis=0, tiled=True)
    all_dy = lax.all_gather(out_grad, "expert", axis=0, tiled=True)
    ids = routing[:, :top].astype(jnp.int32)
    earlier = (jnp.arange(tok)[:, None] < jnp.arange(tok)[None, :]).astype(BF16)
    token_sum = None
    routes, gates, ups, downs = [], [], [], []
    for at in range(local_count):
        expert = lax.axis_index("expert") * local_count + at
        hit = ids == expert
        mine = jnp.any(hit, axis=1)
        weight_of = jnp.sum(jnp.where(hit, routing[:, top:], 0.0), axis=1)
        slot = dot(mine.reshape(groups, tok).astype(BF16), earlier, 1, 0).astype(jnp.int32)
        row_of = (slot + cap * jnp.arange(groups, dtype=jnp.int32)[:, None]).reshape(tokens)
        row_of = jnp.where(mine, row_of, -1)
        match = row_of[:, None] == jnp.arange(rows, dtype=jnp.int32)[None, :]
        pick = match.astype(BF16)
        weights = jnp.sum(jnp.where(match, weight_of[:, None], 0.0), axis=0)[None, :]
        xs = gather_features(dot(all_x, pick, 0, 0, BF16))
        dys = gather_features(dot(all_dy, pick, 0, 0, BF16))
        wg, wu, wd = w_gate[at], w_up[at], w_down[at]
        gate = dot(wg, xs, 1, 0)
        up = dot(wu, xs, 1, 0)
        sig = jax.nn.sigmoid(gate)
        act = gate * sig
        hidden = act * up
        back = dot(wd, dys, 1, 0)
        route_part = jnp.sum(hidden * back, axis=0)
        grad_hidden = weights * back
        d_gate = (grad_hidden * up * sig * (1.0 + gate * (1.0 - sig))).astype(BF16)
        d_up = (grad_hidden * act).astype(BF16)
        scaled = (weights * hidden).astype(BF16)
        both = jnp.concatenate([d_gate, d_up], axis=0)
        w_both = jnp.concatenate([wg, wu], axis=0)
        partial_value = dot(w_both, both, 0, 0, BF16)
        summed = lax.psum_scatter(partial_value, "hidden", scatter_dimension=0, tiled=True)
        placed = dot(pick, summed, 1, 1, F32)
        token_sum = placed if token_sum is None else token_sum + placed
        route = lax.psum(route_part[None, :], "hidden")
        routes.append(jnp.sum(jnp.where(match, route, 0.0), axis=1).reshape(groups, tok))
        downs.append(dot(scaled, dys, 1, 1))
        gates.append(dot(d_gate, xs, 1, 1))
        ups.append(dot(d_up, xs, 1, 1))
    grad_input = lax.psum_scatter(
        token_sum.astype(BF16), "expert", scatter_dimension=0, tiled=True
    )
    sent = jnp.stack(routes, axis=1)
    got = lax.all_to_all(sent, "expert", split_axis=0, concat_axis=0, tiled=True)
    got = got.reshape(experts, tok)
    named = expert_ids[None, :, :] == jnp.arange(experts, dtype=jnp.int32)[:, None, None]
    grad_route = jnp.sum(jnp.where(named, got[:, :, None], 0.0), axis=0)
    return (grad_input, grad_route, jnp.stack(gates), jnp.stack(ups), jnp.stack(downs))


def solution(mesh):
    placed = (
        P("expert", "hidden"),
        P("expert", "hidden"),
        P("expert", None),
        P("expert", None),
        P("expert", "hidden", None),
        P("expert", "hidden", None),
        P("expert", "hidden", None),
    )
    return jax.shard_map(
        per_device,
        mesh=mesh,
        in_specs=placed,
        out_specs=(
            P("expert", "hidden"),
            P("expert", None),
            P("expert", "hidden", None),
            P("expert", "hidden", None),
            P("expert", "hidden", None),
        ),
        check_vma=False,
    )
```
